32 devices in a mesh: enc: 4 (over z), roll: 8 (over y, x, core).
Axes of the slice: x: 2, y: 2, z: 4, core: 2. Of those that a mesh axis runs over, the one named last changes fastest.
Arguments:
- row_grads: bfloat16 [4, 256, 8192], P('enc', 'roll'), may hold values from -1.5 to 1.5
- row_dest: int32 [4, 256], P('enc', 'roll'), may hold values from 0 to 32, as said below
- merger_in: bfloat16 [4, 32, 5120], P('enc'), may hold values from -6 to 6
- hidden_pre: bfloat16 [4, 32, 5120], P('enc'), may hold values from -8 to 8
- w_second: bfloat16 [5120, 8192], P(None, 'roll'), may hold values from -0.125 to 0.125
Outputs:
- pre_grads: bfloat16 [4, 32, 5120], P('enc', None, 'roll')
- grad_first: float32 [5120, 5120], P('enc', 'roll')
- grad_second: float32 [5120, 8192], P('enc', 'roll')
The draws below stay inside these ranges and needn't reach their ends.
Inputs may be any that keep to these rules, and one draw needn't show every extreme that they name: `row_dest`: slot j of rollout device r in a group (slots r * 32 to (r + 1) * 32 - 1) holds 32 for an unused slot or a merged row of its prompt, in [(r // 8) * 32, (r // 8 + 1) * 32); the used rows of one device are distinct.
All inputs are finite; a program needn't handle non-finite values.
Results may differ from the reference program's by a relative error of at most 0.017.
Values may be sent and summed in bfloat16 or wider, within the bound.
No kernel may reach another device: no remote copies, remote signals or barrier semaphores. Data moves between devices by JAX's collectives and lax.ppermute only.
A program may use at most 128 MiB of HBM per device.

```python
import math
import jax
import jax.numpy as jnp
from jax import lax

D = 8192
MW = 5120
ROWS_DEV = 32
GROUPS = 4
SHARDS = 8
ROLLOUTS = 8
MERGED = 32
ROLL_ROWS = 256
ALLROWS = 128


def draw_row_dest(key, part):
    key_order = jax.random.fold_in(key, 11)
    key_live = jax.random.fold_in(key, 23)
    scores = jax.random.randint(key_order, (GROUPS, SHARDS, ROWS_DEV), 0, 1048576)
    within = jnp.arange(ROWS_DEV, dtype=jnp.int32)
    order = jnp.argsort(scores * ROWS_DEV + within[None, None, :], axis=-1).astype(jnp.int32)
    live = jax.random.randint(key_live, (GROUPS, SHARDS), ROWS_DEV // 2, ROWS_DEV + 1)
    shard_ids = jnp.arange(SHARDS, dtype=jnp.int32)
    rollout = shard_ids % ROLLOUTS
    live = jnp.where(rollout[None, :] == 0, ROWS_DEV, jnp.where(rollout[None, :] == ROLLOUTS - 1, ROWS_DEV // 2, live))
    base = shard_ids // ROLLOUTS * ROWS_DEV
    target = base[None, :, None] + order
    dest = jnp.where(within[None, None, :] < live[:, :, None], target, MERGED)
    return dest.reshape(GROUPS, ROLL_ROWS).astype(jnp.int32)


def raised(array, own_key, source, target, parts, factor):
    def block_of(dim):
        return (jnp.arange(array.shape[dim]) // (array.shape[dim] // parts)).reshape((-1,) + (1,) * (array.ndim - 1 - dim))

    first = jax.random.permutation(own_key, parts)[block_of(target)]
    far = (block_of(target) + parts // 2) % parts
    return jnp.where((block_of(source) == first) | (block_of(source) == far), factor * array, array)


def shard_levels(stream_key, extent, shards, least, high):
    def one(axis_at, blocks):
        steps = jax.random.uniform(jax.random.fold_in(jax.random.fold_in(stream_key, 6), axis_at), (blocks,), jnp.float32, least / len(shards), high / len(shards))
        return jnp.repeat(jnp.exp(steps), extent[axis_at] // blocks).reshape((-1,) + (1,) * (len(extent) - axis_at - 1))

    gain = one(*shards[0])
    for cut in shards[1:]:
        gain = gain * one(*cut)
    return gain


def centred(stream_key, dims, spread, limit, shards=(), kind=jnp.bfloat16):
    drawn = spread * jax.random.normal(stream_key, dims, jnp.float32)
    if shards:
        drawn = drawn * shard_levels(stream_key, dims, shards, -0.22, 0.18)
    return jnp.clip(drawn, -limit, limit).astype(kind)


def heavy_noise(rng, dims, deviation, reach, split, heavy, held_as=jnp.bfloat16):
    array = deviation * jax.random.normal(rng, dims, jnp.float32)
    if split:
        array = array * shard_levels(rng, dims, split, -0.22, 0.18)
    return jnp.clip(raised(array, jax.random.fold_in(rng, 3), *heavy), -reach, reach).astype(held_as)


def setup_inputs(seed: int = 0) -> dict:
    seeds = jax.random.split(jax.random.key(seed), 6)
    row_grads = centred(seeds[0], (GROUPS, ROLL_ROWS, D), 0.25, 1.5, ((0, 4), (1, 8)))
    row_dest = draw_row_dest(jax.random.fold_in(seeds[5], 71), 0)
    merger_in = centred(seeds[2], (GROUPS, MERGED, MW), 1.0, 6.0, ((0, 4),))
    hidden_pre = centred(seeds[3], (GROUPS, MERGED, MW), 1.5, 8.0, ((0, 4),))
    w_second = heavy_noise(seeds[4], (MW, D), MW ** -0.5, 0.125, ((1, 8),), (1, 0, 8, 2.0))
    return {"row_grads": row_grads, "row_dest": row_dest, "merger_in": merger_in, "hidden_pre": hidden_pre, "w_second": w_second}


inv_root_two = 1.0 / math.sqrt(2.0)
inv_root_two_pi = 1.0 / math.sqrt(2.0 * math.pi)

def gelu_slope(values):
    return 0.5 * (1.0 + lax.erf(values * inv_root_two)) + values * jnp.exp(-0.5 * values * values) * inv_root_two_pi

def to_bfloat(values):
    return lax.optimization_barrier(values.astype(jnp.bfloat16)).astype(jnp.float32)

def reference(row_grads, row_dest, merger_in, hidden_pre, w_second):
    factor = 1.0 / math.sqrt(ALLROWS)
    grad_first = jnp.zeros((MW, MW), jnp.float32)
    grad_second = jnp.zeros((MW, D), jnp.float32)
    results = []
    for group in range(GROUPS):
        sums = jax.ops.segment_sum(row_grads[group].astype(jnp.float32), row_dest[group].astype(jnp.int32), num_segments=MERGED + 1)[:MERGED]
        merged = sums.astype(jnp.bfloat16)
        before = hidden_pre[group].astype(jnp.float32)
        hidden = jax.nn.gelu(before, approximate=False).astype(jnp.bfloat16)
        units = jnp.dot(merged, w_second.T, preferred_element_type=jnp.float32)
        grads = (units * gelu_slope(before)).astype(jnp.bfloat16)
        results.append(grads)
        term_second = jnp.dot(hidden.T, merged, preferred_element_type=jnp.float32) * factor
        term_first = jnp.dot(merger_in[group].T, grads, preferred_element_type=jnp.float32) * factor
        grad_second = grad_second + to_bfloat(term_second)
        grad_first = grad_first + to_bfloat(term_first)
    return (jnp.stack(results), grad_first, grad_second)
```

```python
import math

import jax
import jax.numpy as jnp
from jax import lax
from jax.sharding import PartitionSpec as P

inv_root_two = 1.0 / math.sqrt(2.0)
inv_root_two_pi = 1.0 / math.sqrt(2.0 * math.pi)


def gelu_slope(values):
    return (
        0.5 * (1.0 + lax.erf(values * inv_root_two))
        + values * jnp.exp(-0.5 * values * values) * inv_root_two_pi
    )


def gather(block, axis):
    copies = jnp.broadcast_to(block[None], (lax.axis_size(axis),) + block.shape)
    return lax.all_to_all(copies, axis, split_axis=0, concat_axis=0, tiled=True)


def body(row_grads, row_dest, merger_in, hidden_pre, w_second):
    slots = row_grads[0]
    slot_count = slots.shape[0]
    merged_count = hidden_pre.shape[1]
    width = hidden_pre.shape[2]
    shards = lax.axis_size("roll")
    groups = lax.axis_size("enc")
    prompts = merged_count // slot_count
    per_prompt = shards // prompts
    columns = slots.shape[1] // shards
    unit_cols = width // shards
    in_cols = width // groups
    shard = lax.axis_index("roll")

    features = jnp.stack([hidden_pre[0], merger_in[0]])
    features = features.reshape(2, merged_count, groups, in_cols).transpose(2, 0, 1, 3)
    features = lax.all_to_all(features, "enc", split_axis=0, concat_axis=0, tiled=True)
    before_all = features[:, 0].reshape(groups * merged_count, in_cols)
    inputs_all = features[:, 1].reshape(groups * merged_count, in_cols)

    local_dest = row_dest[0] - shard // per_prompt * slot_count
    picker = (local_dest[None, :] == jnp.arange(slot_count, dtype=jnp.int32)[:, None]).astype(jnp.bfloat16)
    placed = jnp.einsum(
        "ms,src->rmc", picker, slots.reshape(slot_count, shards, columns),
        preferred_element_type=jnp.float32,
    ).astype(jnp.bfloat16)
    placed = lax.all_to_all(placed, "roll", split_axis=0, concat_axis=0, tiled=True)
    merged = placed.reshape(prompts, per_prompt, slot_count, columns).astype(jnp.float32).sum(1)
    merged = merged.reshape(merged_count, columns).astype(jnp.bfloat16)
    merged_all = gather(merged, "enc").reshape(groups * merged_count, columns)

    partial = jnp.einsum(
        "mc,ruc->rmu", merged, w_second.reshape(shards, unit_cols, columns),
        preferred_element_type=jnp.float32,
    ).astype(jnp.bfloat16)
    partial = lax.all_to_all(partial, "roll", split_axis=0, concat_axis=0, tiled=True)
    units = partial.astype(jnp.float32).sum(0)
    before_part = lax.dynamic_slice_in_dim(hidden_pre[0], shard * unit_cols, unit_cols, 1).astype(jnp.float32)
    grads = (units * gelu_slope(before_part)).astype(jnp.bfloat16)
    grads_all = gather(grads, "enc").reshape(groups * merged_count, unit_cols)

    factor = 1.0 / math.sqrt(merged_count * groups)
    hidden = jax.nn.gelu(before_all.astype(jnp.float32), approximate=False).astype(jnp.bfloat16)
    contract_rows = (((0,), (0,)), ((), ()))
    grad_second = lax.dot_general(hidden, merged_all, contract_rows, preferred_element_type=jnp.float32) * factor
    grad_first = lax.dot_general(inputs_all, grads_all, contract_rows, preferred_element_type=jnp.float32) * factor
    return (grads[None], grad_first, grad_second)


def solution(mesh):
    return jax.shard_map(
        body,
        mesh=mesh,
        in_specs=(
            P("enc", "roll", None),
            P("enc", "roll"),
            P("enc", None, None),
            P("enc", None, None),
            P(None, "roll"),
        ),
        out_specs=(P("enc", None, "roll"), P("enc", "roll"), P("enc", "roll")),
        check_vma=False,
    )
```

```python
import functools
import math

import jax
import jax.numpy as jnp
from jax import lax
from jax.experimental import pallas as pl
from jax.experimental.pallas import tpu as pltpu
from jax.sharding import PartitionSpec as P


inv_root_two = 1.0 / math.sqrt(2.0)
inv_root_two_pi = 1.0 / math.sqrt(2.0 * math.pi)
VMEM = pl.BlockSpec(memory_space=pltpu.VMEM)


def gelu_slope(values):
    return (
        0.5 * (1.0 + lax.erf(values * inv_root_two))
        + values * jnp.exp(-0.5 * values * values) * inv_root_two_pi
    )


def gelu(values):
    return 0.5 * values * (1.0 + lax.erf(values * inv_root_two))


def call(kernel, outs, args, name, flops, limit=8 << 20):
    moved = sum(math.prod(a.shape) * a.dtype.itemsize for a in list(outs) + list(args))
    return pl.pallas_call(
        kernel,
        out_shape=outs,
        in_specs=[VMEM] * len(args),
        out_specs=[VMEM] * len(outs),
        name=name,
        cost_estimate=pl.CostEstimate(flops=flops, bytes_accessed=moved, transcendentals=0),
        compiler_params=pltpu.CompilerParams(vmem_limit_bytes=limit),
    )(*args)


def exchange(block, axis, step):
    pairs = [(i, i ^ step) for i in range(lax.axis_size(axis))]
    return lax.ppermute(block, axis, pairs)


def place_rows(parity, dest_ref, slots_ref, out_ref):
    halves, merged_count, columns = out_ref.shape
    shard = lax.axis_index("roll")
    rows = lax.broadcasted_iota(jnp.int32, (merged_count, slots_ref.shape[0]), 0)
    picker = jnp.where(rows == dest_ref[...], 1.0, 0.0).astype(jnp.bfloat16)
    for j in range(halves):
        first = pl.multiple_of((shard ^ (2 * j + parity)) * columns, columns)
        out_ref[j] = jnp.dot(
            picker, slots_ref[:, pl.ds(first, columns)], preferred_element_type=jnp.float32
        ).astype(jnp.bfloat16)


def pair_sum(kept_ref, came_ref, *out_refs):
    for j, out_ref in enumerate(out_refs):
        out_ref[...] = (kept_ref[j].astype(jnp.float32) + came_ref[j].astype(jnp.float32)).astype(jnp.bfloat16)


def unit_blocks(parity, merged, w_ref, out_ref):
    shard = lax.axis_index("roll")
    halves, _, unit_cols = out_ref.shape
    for j in range(halves):
        first = pl.multiple_of((shard ^ (2 * j + parity)) * unit_cols, unit_cols)
        out_ref[j] = lax.dot_general(
            merged, w_ref[pl.ds(first, unit_cols), :], (((1,), (1,)), ((), ())), preferred_element_type=jnp.float32
        ).astype(jnp.bfloat16)


def first_units(parity, *refs):
    *piece_refs, w_ref, merged_ref, out_ref = refs
    total = piece_refs[0][...].astype(jnp.float32)
    for piece_ref in piece_refs[1:]:
        total = total + piece_ref[...].astype(jnp.float32)
    merged_ref[...] = total.astype(jnp.bfloat16)
    unit_blocks(parity, merged_ref[...], w_ref, out_ref)


def second_units(parity, merged_ref, w_ref, out_ref):
    unit_blocks(parity, merged_ref[...], w_ref, out_ref)


def feature_blocks(before_ref, inputs_ref, *out_refs):
    rows = before_ref.shape[0]
    columns = out_refs[0].shape[1]
    group = lax.axis_index("enc")
    for k, out_ref in enumerate(out_refs):
        first = pl.multiple_of((group ^ k) * columns, columns)
        out_ref[:rows, :] = before_ref[:, pl.ds(first, columns)]
        out_ref[rows:, :] = inputs_ref[:, pl.ds(first, columns)]


def outer_sum(count, activate, factor, *refs):
    left_refs, right_refs, out_ref = refs[:count], refs[count:-1], refs[-1]
    left = jnp.concatenate([ref[...] for ref in left_refs], axis=0)
    if activate:
        left = gelu(left.astype(jnp.float32)).astype(jnp.bfloat16)
    right = jnp.concatenate([ref[...] for ref in right_refs], axis=0)
    out_ref[...] = lax.dot_general(
        left, right, (((0,), (0,)), ((), ())), preferred_element_type=jnp.float32
    ) * factor


def row_block(rows):
    for size in (256, 128):
        if rows % size == 0:
            return size
    return rows


def outer(features, half, rights, activate, factor, name):
    rows = rights[0].shape[0]
    in_cols, columns = features[0].shape[1], rights[0].shape[1]
    count = len(rights)
    block = row_block(in_cols)
    flops = 2 * count * rows * in_cols * columns
    moved = 4 * in_cols * columns + 2 * count * rows * (in_cols + columns)
    return pl.pallas_call(
        functools.partial(outer_sum, count, activate, factor),
        grid=(in_cols // block,),
        out_shape=jax.ShapeDtypeStruct((in_cols, columns), jnp.float32),
        in_specs=[pl.BlockSpec((rows, block), lambda i: (half, i))] * count
        + [pl.BlockSpec((rows, columns), lambda i: (0, 0))] * count,
        out_specs=pl.BlockSpec((block, columns), lambda i: (i, 0)),
        name=name,
        cost_estimate=pl.CostEstimate(flops=flops, bytes_accessed=moved, transcendentals=0),
        compiler_params=pltpu.CompilerParams(vmem_limit_bytes=16 << 20),
    )(*features, *rights)


def body(row_grads, row_dest, merger_in, hidden_pre, w_second):
    slots = row_grads[0]
    slot_count = slots.shape[0]
    before, inputs = hidden_pre[0], merger_in[0]
    merged_count, width = before.shape
    shards = lax.axis_size("roll")
    groups = lax.axis_size("enc")
    halves = shards // 2
    columns = slots.shape[1] // shards
    unit_cols = width // shards
    in_cols = width // groups
    shard = lax.axis_index("roll")
    half_type = jnp.bfloat16
    shape = jax.ShapeDtypeStruct

    def scatter_pairs(kept, came, name):
        outs = [shape(kept.shape[1:], half_type)] * halves
        return call(pair_sum, outs, (kept, came), name, kept.size)

    def spread(blocks):
        return [blocks[0]] + [exchange(blocks[j], "roll", 2 * j) for j in range(1, halves)]

    def gather(block):
        return [block] + [exchange(block, "enc", k) for k in range(1, groups)]

    if in_cols % 128 == 0:
        blocks = call(feature_blocks, [shape((2 * merged_count, in_cols), half_type)] * groups, (before, inputs), "features", 0)
    else:
        both = jnp.concatenate([before, inputs], axis=0)
        blocks = [
            lax.dynamic_slice_in_dim(both, (lax.axis_index("enc") ^ k) * in_cols, in_cols, 1) for k in range(groups)
        ]

    place = (halves, merged_count, columns)
    place_flops = 2 * slot_count * math.prod(place)
    dest = row_dest
    (sent,) = call(functools.partial(place_rows, 1), [shape(place, half_type)], (dest, slots), "place_sent", place_flops)
    (kept,) = call(functools.partial(place_rows, 0), [shape(place, half_type)], (dest, slots), "place_kept", place_flops)
    pieces = spread(scatter_pairs(kept, exchange(sent, "roll", 1), "row_pairs"))
    features = [blocks[0]] + [exchange(blocks[k], "enc", k) for k in range(1, groups)]

    unit_shape = (halves, merged_count, unit_cols)
    unit_flops = 2 * columns * math.prod(unit_shape)
    limit = (12 << 20) + 4 * w_second.size
    merged, sent = call(
        functools.partial(first_units, 1),
        [shape((merged_count, columns), half_type), shape(unit_shape, half_type)],
        (*pieces, w_second), "units_sent", unit_flops, limit,
    )
    (kept,) = call(
        functools.partial(second_units, 0), [shape(unit_shape, half_type)], (merged, w_second), "units_kept", unit_flops, limit
    )
    pieces = spread(scatter_pairs(kept, exchange(sent, "roll", 1), "unit_pairs"))
    merged_all = gather(merged)
    slope = gelu_slope(lax.dynamic_slice_in_dim(before, shard * unit_cols, unit_cols, 1).astype(jnp.float32))
    units = sum(piece.astype(jnp.float32) for piece in pieces)
    grads = (units * slope).astype(jnp.bfloat16)
    grads_all = gather(grads)

    factor = 1.0 / math.sqrt(merged_count * groups)
    grad_second = outer(features, 0, merged_all, True, factor, "grad_second")
    grad_first = outer(features, 1, grads_all, False, factor, "grad_first")
    return (grads[None], grad_first, grad_second)


def solution(mesh):
    return jax.shard_map(
        body,
        mesh=mesh,
        in_specs=(
            P("enc", "roll", None),
            P("enc", "roll"),
            P("enc", None, None),
            P("enc", None, None),
            P(None, "roll"),
        ),
        out_specs=(P("enc", None, "roll"), P("enc", "roll"), P("enc", "roll")),
        check_vma=False,
    )
```

```python
import functools
import math

import jax
import jax.numpy as jnp
from jax import lax
from jax.experimental import pallas as pl
from jax.experimental.pallas import tpu as pltpu
from jax.sharding import PartitionSpec as P


inv_root_two = 1.0 / math.sqrt(2.0)
inv_root_two_pi = 1.0 / math.sqrt(2.0 * math.pi)
VMEM = pl.BlockSpec(memory_space=pltpu.VMEM)
HBM = pl.BlockSpec(memory_space=pltpu.HBM)
shape = jax.ShapeDtypeStruct


def gelu_slope(values):
    return (
        0.5 * (1.0 + lax.erf(values * inv_root_two))
        + values * jnp.exp(-0.5 * values * values) * inv_root_two_pi
    )


def gelu(values):
    return 0.5 * values * (1.0 + lax.erf(values * inv_root_two))


def call(kernel, outs, args, flops=0, in_specs=None, out_specs=None, scratch=(), limit=4 << 20):
    moved = sum(math.prod(a.shape) * a.dtype.itemsize for a in list(outs) + list(args))
    return pl.pallas_call(
        kernel,
        out_shape=outs,
        in_specs=in_specs or [VMEM] * len(args),
        out_specs=out_specs or [VMEM] * len(outs),
        scratch_shapes=scratch,
        cost_estimate=pl.CostEstimate(flops=flops, bytes_accessed=moved, transcendentals=0),
        compiler_params=pltpu.CompilerParams(vmem_limit_bytes=limit),
    )(*args)


def exchange(block, axis, step):
    pairs = [(i, i ^ step) for i in range(lax.axis_size(axis))]
    return lax.ppermute(block, axis, pairs)


def place_rows(parity, dest_ref, slots_ref, out_ref, held_dest, held, sems):
    halves, merged_count, columns = out_ref.shape
    shard = lax.axis_index("roll")
    dest_copy = pltpu.make_async_copy(dest_ref, held_dest, sems.at[halves])
    dest_copy.start()
    copies = []
    for j in range(halves):
        first = pl.multiple_of((shard ^ (2 * j + parity)) * columns, columns)
        copies.append(pltpu.make_async_copy(slots_ref.at[:, pl.ds(first, columns)], held.at[j], sems.at[j]))
        copies[-1].start()
    dest_copy.wait()
    rows = lax.broadcasted_iota(jnp.int32, (merged_count, held.shape[1]), 0)
    picker = jnp.where(rows == held_dest[...], 1.0, 0.0).astype(jnp.bfloat16)
    for j in range(halves):
        copies[j].wait()
        out_ref[j] = jnp.dot(picker, held[j], preferred_element_type=jnp.float32).astype(jnp.bfloat16)


def pair_sum(kept_ref, came_ref, *out_refs):
    for j, out_ref in enumerate(out_refs):
        out_ref[...] = (kept_ref[j].astype(jnp.float32) + came_ref[j].astype(jnp.float32)).astype(jnp.bfloat16)


def weight_copies(parity, w_ref, held, sems):
    halves, unit_cols, _ = held.shape
    shard = lax.axis_index("roll")
    copies = []
    for j in range(halves):
        first = pl.multiple_of((shard ^ (2 * j + parity)) * unit_cols, unit_cols)
        copies.append(pltpu.make_async_copy(w_ref.at[pl.ds(first, unit_cols), :], held.at[j], sems.at[j]))
        copies[-1].start()
    return copies


def unit_blocks(copies, merged, held, out_ref):
    for j, copy in enumerate(copies):
        copy.wait()
        out_ref[j] = lax.dot_general(
            merged, held[j], (((1,), (1,)), ((), ())), preferred_element_type=jnp.float32
        ).astype(jnp.bfloat16)


def first_units(parity, *refs):
    *piece_refs, w_ref, merged_ref, out_ref, held, sems = refs
    copies = weight_copies(parity, w_ref, held, sems)
    total = piece_refs[0][...].astype(jnp.float32)
    for piece_ref in piece_refs[1:]:
        total = total + piece_ref[...].astype(jnp.float32)
    merged = total.astype(jnp.bfloat16)
    for k in range(merged_ref.shape[0]):
        merged_ref[k] = merged
    unit_blocks(copies, merged, held, out_ref)


def second_units(parity, merged_ref, w_ref, out_ref, held, sems):
    unit_blocks(weight_copies(parity, w_ref, held, sems), merged_ref[0], held, out_ref)


def feature_blocks(before_ref, inputs_ref, *refs):
    *out_refs, held, sems = refs
    rows = before_ref.shape[0]
    columns = out_refs[0].shape[1]
    group = lax.axis_index("enc")
    copies = []
    for k, out_ref in enumerate(out_refs):
        cut = pl.ds(pl.multiple_of((group ^ k) * columns, columns), columns)
        copies.append((
            pltpu.make_async_copy(before_ref.at[:, cut], held.at[k], sems.at[0, k]),
            pltpu.make_async_copy(inputs_ref.at[:, cut], out_ref.at[pl.ds(rows, rows), :], sems.at[1, k]),
        ))
        for copy in copies[-1]:
            copy.start()
    for k, out_ref in enumerate(out_refs):
        copies[k][0].wait()
        out_ref[:rows, :] = gelu(held[k].astype(jnp.float32)).astype(jnp.bfloat16)
    for _, copy in copies:
        copy.wait()


def slope_block(before_ref, out_ref):
    out_ref[...] = gelu_slope(before_ref[...].astype(jnp.float32))


def write_products(left_of, right, factor, out_ref, held, sems):
    size = held.shape[1]
    copies = []
    for j in range(held.shape[0]):
        held[j] = lax.dot_general(
            left_of(j * size, size), right, (((0,), (0,)), ((), ())), preferred_element_type=jnp.float32
        ) * factor
        copies.append(pltpu.make_async_copy(held.at[j], out_ref.at[pl.ds(j * size, size), :], sems.at[j]))
        copies[-1].start()
    for copy in copies:
        copy.wait()


def second_products(factor, groups, *refs):
    feature_refs, (merged_ref, out_ref, held, sems) = refs[:groups], refs[groups:]
    rows = merged_ref.shape[1]
    group = lax.axis_index("enc")

    def left_of(first, size):
        return jnp.concatenate([ref[:rows, first : first + size] for ref in feature_refs], axis=0)

    right = jnp.concatenate([merged_ref[group ^ k] for k in range(groups)], axis=0)
    write_products(left_of, right, factor, out_ref, held, sems)


def first_products(factor, groups, *refs):
    feature_refs, grad_refs, (out_ref, held, sems) = refs[:groups], refs[groups : 2 * groups], refs[2 * groups :]
    rows = grad_refs[0].shape[0]

    def left_of(first, size):
        return jnp.concatenate([ref[rows:, first : first + size] for ref in feature_refs], axis=0)

    right = jnp.concatenate([ref[...] for ref in grad_refs], axis=0)
    write_products(left_of, right, factor, out_ref, held, sems)


def products(kernel, factor, features, rights, columns):
    groups, (rows, in_cols) = len(features), features[0].shape
    size = next((s for s in (256, 128) if in_cols % s == 0), in_cols)
    out = shape((in_cols, columns), jnp.float32)
    (result,) = call(
        functools.partial(kernel, factor, groups), [out], (*features, *rights), groups * rows * in_cols * columns,
        out_specs=[HBM],
        scratch=[pltpu.VMEM((in_cols // size, size, columns), jnp.float32), pltpu.SemaphoreType.DMA((in_cols // size,))],
        limit=(6 << 20) + 4 * in_cols * columns,
    )
    return result


def body(row_grads, row_dest, merger_in, hidden_pre, w_second):
    slots = row_grads[0]
    slot_count = slots.shape[0]
    before, inputs = hidden_pre[0], merger_in[0]
    merged_count, width = before.shape
    slots, row_dest, w_second = (pltpu.with_memory_space_constraint(x, pltpu.HBM) for x in (slots, row_dest, w_second))
    shards = lax.axis_size("roll")
    groups = lax.axis_size("enc")
    halves = shards // 2
    columns = slots.shape[1] // shards
    unit_cols = width // shards
    in_cols = width // groups
    shard = lax.axis_index("roll")
    kind = jnp.bfloat16

    def spread(kept, came):
        blocks = call(pair_sum, [shape(kept.shape[1:], kind)] * halves, (kept, came), kept.size)
        return [blocks[0]] + [exchange(blocks[j], "roll", 2 * j) for j in range(1, halves)]

    if in_cols % 128 == 0:
        outs = [shape((2 * merged_count, in_cols), kind)] * groups
        scratch = [pltpu.VMEM((groups, merged_count, in_cols), kind), pltpu.SemaphoreType.DMA((2, groups))]
        sources = [pltpu.with_memory_space_constraint(x, pltpu.HBM) for x in (before, inputs)]
        blocks = call(feature_blocks, outs, sources, in_specs=[HBM, HBM], scratch=scratch, limit=8 << 20)
    else:
        both = jnp.concatenate([gelu(before.astype(jnp.float32)).astype(kind), inputs], axis=0)
        group = lax.axis_index("enc")
        blocks = [lax.dynamic_slice_in_dim(both, (group ^ k) * in_cols, in_cols, 1) for k in range(groups)]
    features = [blocks[0]] + [exchange(blocks[k], "enc", k) for k in range(1, groups)]

    place = (halves, merged_count, columns)

    def placed(parity):
        scratch = [
            pltpu.VMEM(row_dest.shape, row_dest.dtype),
            pltpu.VMEM((halves, slot_count, columns), kind),
            pltpu.SemaphoreType.DMA((halves + 1,)),
        ]
        return call(
            functools.partial(place_rows, parity), [shape(place, kind)], (row_dest, slots),
            2 * slot_count * math.prod(place), in_specs=[HBM, HBM], scratch=scratch, limit=8 << 20,
        )[0]

    came = exchange(placed(1), "roll", 1)
    pieces = spread(placed(0), came)

    unit_shape = (halves, merged_count, unit_cols)
    flops = 2 * columns * math.prod(unit_shape)
    scratch = [pltpu.VMEM((halves, unit_cols, columns), kind), pltpu.SemaphoreType.DMA((halves,))]
    limit = (8 << 20) + w_second.size
    copies, sent = call(
        functools.partial(first_units, 1),
        [shape((groups, merged_count, columns), kind), shape(unit_shape, kind)],
        (*pieces, w_second), flops, in_specs=[VMEM] * halves + [HBM], scratch=scratch, limit=limit,
    )
    came = exchange(sent, "roll", 1)
    (kept,) = call(
        functools.partial(second_units, 0), [shape(unit_shape, kind)], (copies, w_second), flops,
        in_specs=[VMEM, HBM], scratch=scratch, limit=limit,
    )
    pieces = spread(kept, came)
    merged_all = lax.all_to_all(copies, "enc", split_axis=0, concat_axis=0, tiled=True)
    own = lax.dynamic_slice_in_dim(before, shard * unit_cols, unit_cols, 1)
    (slope,) = call(slope_block, [shape(own.shape, jnp.float32)], (own,))
    grads = (sum(piece.astype(jnp.float32) for piece in pieces) * slope).astype(kind)
    grads_all = [grads] + [exchange(grads, "enc", k) for k in range(1, groups)]

    factor = 1.0 / math.sqrt(merged_count * groups)
    grad_second = products(second_products, factor, features, [merged_all], columns)
    grad_first = products(first_products, factor, features, grads_all, unit_cols)
    return (grads[None], grad_first, grad_second)


def solution(mesh):
    return jax.shard_map(
        body,
        mesh=mesh,
        in_specs=(
            P("enc", "roll", None),
            P("enc", "roll"),
            P("enc", None, None),
            P("enc", None, None),
            P(None, "roll"),
        ),
        out_specs=(P("enc", None, "roll"), P("enc", "roll"), P("enc", "roll")),
        check_vma=False,
    )
```

```python
import functools
import math

import jax
import jax.numpy as jnp
from jax import lax
from jax.experimental import pallas as pl
from jax.experimental.pallas import tpu as pltpu
from jax.sharding import PartitionSpec as P


inv_root_two = 1.0 / math.sqrt(2.0)
inv_root_two_pi = 1.0 / math.sqrt(2.0 * math.pi)
VMEM = pl.BlockSpec(memory_space=pltpu.VMEM)
HBM = pl.BlockSpec(memory_space=pltpu.HBM)
shape = jax.ShapeDtypeStruct


def gelu_slope(values):
    return (
        0.5 * (1.0 + lax.erf(values * inv_root_two))
        + values * jnp.exp(-0.5 * values * values) * inv_root_two_pi
    )


def gelu(values):
    return 0.5 * values * (1.0 + lax.erf(values * inv_root_two))


def call(kernel, outs, args, flops=0, in_specs=None, out_specs=None, scratch=(), limit=4 << 20):
    moved = sum(math.prod(a.shape) * a.dtype.itemsize for a in list(outs) + list(args))
    return pl.pallas_call(
        kernel,
        out_shape=outs,
        in_specs=in_specs or [VMEM] * len(args),
        out_specs=out_specs or [VMEM] * len(outs),
        scratch_shapes=scratch,
        cost_estimate=pl.CostEstimate(flops=flops, bytes_accessed=moved, transcendentals=0),
        compiler_params=pltpu.CompilerParams(vmem_limit_bytes=limit),
    )(*args)


def exchange(block, axis, step):
    pairs = [(i, i ^ step) for i in range(lax.axis_size(axis))]
    return lax.ppermute(block, axis, pairs)


def front(halves, groups, aligned, *refs):
    dest_ref, slots_ref, before_ref, inputs_ref = refs[:4]
    placed_refs, rest = refs[4:6], refs[6:]
    feature_refs = rest[: groups * aligned]
    slope_refs = rest[groups * aligned : (groups + 1) * aligned]
    held_dest, held, held_before, held_own, sems = rest[(groups + 1) * aligned :]
    _, merged_count, columns = placed_refs[0].shape
    shard, group = lax.axis_index("roll"), lax.axis_index("enc")
    started = iter(range(sems.shape[0]))

    def fetch(source, target):
        copy = pltpu.make_async_copy(source, target, sems.at[next(started)])
        copy.start()
        return copy

    def cut(index, size):
        return pl.ds(pl.multiple_of(index * size, size), size)

    dest_copy = fetch(dest_ref, held_dest)
    slot_copies = [
        fetch(slots_ref.at[:, cut(shard ^ (2 * j + parity), columns)], held.at[parity, j])
        for parity in (1, 0)
        for j in range(halves)
    ]
    before_copies, input_copies = [], []
    for k, ref in enumerate(feature_refs):
        size = ref.shape[1]
        before_copies.append(fetch(before_ref.at[:, cut(group ^ k, size)], held_before.at[k]))
        input_copies.append(
            fetch(inputs_ref.at[:, cut(group ^ k, size)], ref.at[pl.ds(merged_count, merged_count), :])
        )
    own_copies = [fetch(before_ref.at[:, cut(shard, ref.shape[1])], held_own) for ref in slope_refs]
    dest_copy.wait()
    rows = lax.broadcasted_iota(jnp.int32, (merged_count, held.shape[2]), 0)
    picker = jnp.where(rows == held_dest[...], 1.0, 0.0).astype(jnp.bfloat16)
    slot_copies = iter(slot_copies)
    for parity in (1, 0):
        for j in range(halves):
            next(slot_copies).wait()
            placed_refs[parity][j] = jnp.dot(
                picker, held[parity, j], preferred_element_type=jnp.float32
            ).astype(jnp.bfloat16)
    for k, copy in enumerate(before_copies):
        copy.wait()
        feature_refs[k][:merged_count, :] = gelu(held_before[k].astype(jnp.float32)).astype(jnp.bfloat16)
    for ref, copy in zip(slope_refs, own_copies):
        copy.wait()
        ref[...] = gelu_slope(held_own[...].astype(jnp.float32))
    for copy in input_copies:
        copy.wait()


def load(source_ref, out_ref, sems):
    size = source_ref.shape[0] // sems.shape[0]
    copies = []
    for j in range(sems.shape[0]):
        cut = pl.ds(j * size, size)
        copies.append(pltpu.make_async_copy(source_ref.at[cut, :], out_ref.at[cut, :], sems.at[j]))
        copies[-1].start()
    for copy in copies:
        copy.wait()


def join(*refs):
    *piece_refs, out_ref = refs
    first = 0
    for ref in piece_refs:
        out_ref[first : first + ref.shape[0], :] = ref[...]
        first += ref.shape[0]


def pair_sum(kept_ref, came_ref, *out_refs):
    for j, out_ref in enumerate(out_refs):
        out_ref[...] = (kept_ref[j].astype(jnp.float32) + came_ref[j].astype(jnp.float32)).astype(jnp.bfloat16)


def unit_blocks(parity, merged, w_ref, out_ref):
    shard = lax.axis_index("roll")
    halves, _, unit_cols = out_ref.shape
    for j in range(halves):
        first = pl.multiple_of((shard ^ (2 * j + parity)) * unit_cols, unit_cols)
        out_ref[j] = lax.dot_general(
            merged, w_ref[pl.ds(first, unit_cols), :], (((1,), (1,)), ((), ())), preferred_element_type=jnp.float32
        ).astype(jnp.bfloat16)


def first_units(*refs):
    *piece_refs, w_ref, merged_ref, out_ref = refs
    total = piece_refs[0][...].astype(jnp.float32)
    for piece_ref in piece_refs[1:]:
        total = total + piece_ref[...].astype(jnp.float32)
    merged_ref[...] = total.astype(jnp.bfloat16)
    unit_blocks(1, merged_ref[...], w_ref, out_ref)


def second_units(merged_ref, w_ref, out_ref):
    unit_blocks(0, merged_ref[...], w_ref, out_ref)


def write_products(left_of, right, factor, out_ref, held, sems):
    size = held.shape[1]
    copies = []
    for j in range(held.shape[0]):
        held[j] = lax.dot_general(
            left_of(j * size, size), right, (((0,), (0,)), ((), ())), preferred_element_type=jnp.float32
        ) * factor
        copies.append(pltpu.make_async_copy(held.at[j], out_ref.at[pl.ds(j * size, size), :], sems.at[j]))
        copies[-1].start()
    for copy in copies:
        copy.wait()


def block_products(part, factor, groups, *refs):
    feature_refs, right_refs, (out_ref, held, sems) = refs[:groups], refs[groups:-3], refs[-3:]
    rows = feature_refs[0].shape[0] // 2
    half = slice(part * rows, (part + 1) * rows)

    def left_of(first, size):
        return jnp.concatenate([ref[half, first : first + size] for ref in feature_refs], axis=0)

    right = jnp.concatenate([ref[...] for ref in right_refs], axis=0)
    write_products(left_of, right, factor, out_ref, held, sems)


def products(part, factor, features, rights, columns):
    groups, (rows, in_cols) = len(features), features[0].shape
    size = next((s for s in (256, 128) if in_cols % s == 0), in_cols)
    out = shape((in_cols, columns), jnp.float32)
    (result,) = call(
        functools.partial(block_products, part, factor, groups), [out], (*features, *rights), groups * rows * in_cols * columns,
        out_specs=[HBM],
        scratch=[pltpu.VMEM((in_cols // size, size, columns), jnp.float32), pltpu.SemaphoreType.DMA((in_cols // size,))],
        limit=(6 << 20) + 4 * in_cols * columns,
    )
    return result


def body(row_grads, row_dest, merger_in, hidden_pre, w_second):
    slots = row_grads[0]
    slot_count = slots.shape[0]
    before, inputs = hidden_pre[0], merger_in[0]
    merged_count, width = before.shape
    shards = lax.axis_size("roll")
    groups = lax.axis_size("enc")
    halves = shards // 2
    columns = slots.shape[1] // shards
    unit_cols = width // shards
    in_cols = width // groups
    kind = jnp.bfloat16
    aligned = in_cols % 128 == 0 and unit_cols % 128 == 0

    def spread(kept, came):
        blocks = call(pair_sum, [shape(kept.shape[1:], kind)] * halves, (kept, came), kept.size)
        return [blocks[0]] + [exchange(blocks[j], "roll", 2 * j) for j in range(1, halves)]

    place = (halves, merged_count, columns)
    outs = [shape(place, kind)] * 2
    if aligned:
        outs += [shape((2 * merged_count, in_cols), kind)] * groups + [shape((merged_count, unit_cols), jnp.float32)]
    sources = [pltpu.with_memory_space_constraint(x, pltpu.HBM) for x in (row_dest, slots, before, inputs)]
    scratch = [
        pltpu.VMEM(row_dest.shape, row_dest.dtype),
        pltpu.VMEM((2, halves, slot_count, columns), kind),
        pltpu.VMEM((groups, merged_count, in_cols), kind),
        pltpu.VMEM((merged_count, unit_cols), kind),
        pltpu.SemaphoreType.DMA((2 + 2 * halves + 2 * groups,)),
    ]
    kept, sent, *rest = call(
        functools.partial(front, halves, groups, int(aligned)), outs, sources,
        2 * slot_count * slots.size, in_specs=[HBM] * 4, scratch=scratch, limit=12 << 20,
    )
    if aligned:
        *blocks, slope = rest
    else:
        both = jnp.concatenate([gelu(before.astype(jnp.float32)).astype(kind), inputs], axis=0)
        group = lax.axis_index("enc")
        blocks = [lax.dynamic_slice_in_dim(both, (group ^ k) * in_cols, in_cols, 1) for k in range(groups)]
        own = lax.dynamic_slice_in_dim(before, lax.axis_index("roll") * unit_cols, unit_cols, 1)
        slope = gelu_slope(own.astype(jnp.float32))
    features = [blocks[0]] + [exchange(blocks[k], "enc", k) for k in range(1, groups)]

    pieces = spread(kept, exchange(sent, "roll", 1))
    (weights,) = call(
        load, [shape(w_second.shape, kind)], (pltpu.with_memory_space_constraint(w_second, pltpu.HBM),),
        in_specs=[HBM], scratch=[pltpu.SemaphoreType.DMA((8,))],
    )

    unit_shape = (halves, merged_count, unit_cols)
    flops = 2 * columns * math.prod(unit_shape)
    merged, sent = call(
        first_units, [shape((merged_count, columns), kind), shape(unit_shape, kind)], (*pieces, weights), flops,
    )
    came = exchange(sent, "roll", 1)
    (kept,) = call(second_units, [shape(unit_shape, kind)], (merged, weights), flops)

    merged_all = [merged]
    step = 1
    while step < groups:
        (whole,) = merged_all if step == 1 else call(join, [shape((step * merged_count, columns), kind)], merged_all)
        merged_all = [whole, exchange(whole, "enc", step)]
        step *= 2

    pieces = spread(kept, came)
    grads = (sum(piece.astype(jnp.float32) for piece in pieces) * slope).astype(kind)
    grads_all = [grads] + [exchange(grads, "enc", k) for k in range(1, groups)]

    factor = 1.0 / math.sqrt(merged_count * groups)
    grad_second = products(0, factor, features, merged_all, columns)
    grad_first = products(1, factor, features, grads_all, unit_cols)
    return (grads[None], grad_first, grad_second)


def solution(mesh):
    return jax.shard_map(
        body,
        mesh=mesh,
        in_specs=(
            P("enc", "roll", None),
            P("enc", "roll"),
            P("enc", None, None),
            P("enc", None, None),
            P(None, "roll"),
        ),
        out_specs=(P("enc", None, "roll"), P("enc", "roll"), P("enc", "roll")),
        check_vma=False,
    )
```

```python
import functools
import math

import jax
import jax.numpy as jnp
from jax import lax
from jax.experimental import pallas as pl
from jax.experimental.pallas import tpu as pltpu
from jax.sharding import PartitionSpec as P


inv_root_two = 1.0 / math.sqrt(2.0)
inv_root_two_pi = 1.0 / math.sqrt(2.0 * math.pi)
VMEM = pl.BlockSpec(memory_space=pltpu.VMEM)
HBM = pl.BlockSpec(memory_space=pltpu.HBM)
shape = jax.ShapeDtypeStruct


def gelu_slope(values):
    return (
        0.5 * (1.0 + lax.erf(values * inv_root_two))
        + values * jnp.exp(-0.5 * values * values) * inv_root_two_pi
    )


def gelu(values):
    return 0.5 * values * (1.0 + lax.erf(values * inv_root_two))


def call(kernel, outs, args, flops=0, in_specs=None, out_specs=None, scratch=(), limit=4 << 20):
    moved = sum(math.prod(a.shape) * a.dtype.itemsize for a in list(outs) + list(args))
    return pl.pallas_call(
        kernel,
        out_shape=outs,
        in_specs=in_specs or [VMEM] * len(args),
        out_specs=out_specs or [VMEM] * len(outs),
        scratch_shapes=scratch,
        cost_estimate=pl.CostEstimate(flops=flops, bytes_accessed=moved, transcendentals=0),
        compiler_params=pltpu.CompilerParams(vmem_limit_bytes=limit),
    )(*args)


def exchange(block, axis, step):
    pairs = [(i, i ^ step) for i in range(lax.axis_size(axis))]
    return lax.ppermute(block, axis, pairs)


def feature_cuts(groups):
    lane = lax.axis_index("roll") % 2
    return [(0, None)] + [(k + lane, None) for k in range(1, groups - 1, 2)] + [(groups - 1, lane)]


def front(halves, groups, aligned, *refs):
    dest_ref, slots_ref, before_ref, inputs_ref = refs[:4]
    placed_refs, rest = refs[4:6], refs[6:]
    count = groups // 2 + 1
    feature_refs = rest[: count * aligned]
    slope_refs = rest[count * aligned : (count + 1) * aligned]
    held_dest, held, held_own, sems = rest[(count + 1) * aligned :]
    _, merged_count, columns = placed_refs[0].shape
    shard, group = lax.axis_index("roll"), lax.axis_index("enc")
    started = iter(range(sems.shape[0]))

    def fetch(source, target):
        copy = pltpu.make_async_copy(source, target, sems.at[next(started)])
        copy.start()
        return copy

    def cut(index, size):
        return pl.ds(pl.multiple_of(index * size, size), size)

    dest_copy = fetch(dest_ref, held_dest)
    spots = [2 * j + parity for parity in (1, 0) for j in range(halves)]
    slot_copies = [
        fetch(slots_ref.at[:, cut(shard ^ k, columns)], held.at[:, pl.ds(i * columns, columns)]) for i, k in enumerate(spots)
    ]
    before_copies, input_copies = [], []
    for ref, (distance, half) in zip(feature_refs, feature_cuts(groups)):
        index = group ^ distance
        source = cut(index if half is None else 2 * index + half, ref.shape[1])
        before_copies.append(fetch(before_ref.at[:, source], ref.at[pl.ds(0, merged_count), :]))
        input_copies.append(fetch(inputs_ref.at[:, source], ref.at[pl.ds(merged_count, merged_count), :]))
    own_copies = [fetch(before_ref.at[:, cut(shard, ref.shape[1])], held_own) for ref in slope_refs]
    dest_copy.wait()
    rows = lax.broadcasted_iota(jnp.int32, (merged_count, held.shape[0]), 0)
    picker = jnp.where(rows == held_dest[...], 1.0, 0.0).astype(jnp.bfloat16)
    for copy in slot_copies:
        copy.wait()
    placed = jnp.dot(picker, held[...], preferred_element_type=jnp.float32).astype(jnp.bfloat16)
    for i, k in enumerate(spots):
        placed_refs[k % 2][k // 2] = placed[:, i * columns : (i + 1) * columns]
    for ref, copy in zip(slope_refs, own_copies):
        copy.wait()
        ref[...] = gelu_slope(held_own[...].astype(jnp.float32))
    for copy in before_copies + input_copies:
        copy.wait()


def load(source_ref, out_ref, sems):
    size = source_ref.shape[0] // sems.shape[0]
    copies = []
    for j in range(sems.shape[0]):
        cut = pl.ds(j * size, size)
        copies.append(pltpu.make_async_copy(source_ref.at[cut, :], out_ref.at[cut, :], sems.at[j]))
        copies[-1].start()
    for copy in copies:
        copy.wait()


def join(*refs):
    *piece_refs, out_ref = refs
    first = 0
    for ref in piece_refs:
        out_ref[first : first + ref.shape[0], :] = ref[...]
        first += ref.shape[0]


def pair_sum(kept_ref, came_ref, *out_refs):
    for j, out_ref in enumerate(out_refs):
        out_ref[...] = (kept_ref[j].astype(jnp.float32) + came_ref[j].astype(jnp.float32)).astype(jnp.bfloat16)


def unit_blocks(parity, merged, w_ref, out_ref):
    shard = lax.axis_index("roll")
    halves, _, unit_cols = out_ref.shape
    for j in range(halves):
        first = pl.multiple_of((shard ^ (2 * j + parity)) * unit_cols, unit_cols)
        out_ref[j] = lax.dot_general(
            merged, w_ref[pl.ds(first, unit_cols), :], (((1,), (1,)), ((), ())), preferred_element_type=jnp.float32
        ).astype(jnp.bfloat16)


def first_units(*refs):
    *piece_refs, w_ref, merged_ref, out_ref = refs
    total = piece_refs[0][...].astype(jnp.float32)
    for piece_ref in piece_refs[1:]:
        total = total + piece_ref[...].astype(jnp.float32)
    merged_ref[...] = total.astype(jnp.bfloat16)
    unit_blocks(1, merged_ref[...], w_ref, out_ref)


def second_units(merged_ref, w_ref, out_ref):
    unit_blocks(0, merged_ref[...], w_ref, out_ref)


def write_products(left_of, right, factor, out_ref, held, sems):
    size = held.shape[1]
    copies = []
    for j in range(held.shape[0]):
        held[j] = lax.dot_general(
            left_of(j * size, size), right, (((0,), (0,)), ((), ())), preferred_element_type=jnp.float32
        ) * factor
        copies.append(pltpu.make_async_copy(held.at[j], out_ref.at[pl.ds(j * size, size), :], sems.at[j]))
        copies[-1].start()
    for copy in copies:
        copy.wait()


def block_products(part, factor, places, *refs):
    groups = len(places)
    feature_refs, right_refs, (out_ref, held, sems) = refs[: groups + 1], refs[groups + 1 : -3], refs[-3:]
    *whole_refs, mine_ref, came_ref = feature_refs
    rows = mine_ref.shape[0] // 2
    rows_cut = slice(part * rows, (part + 1) * rows)
    half_cols = mine_ref.shape[1]
    lane = lax.axis_index("roll") % 2

    def left_of(first, size):
        half, start = divmod(first, half_cols)
        pieces = [ref[rows_cut, first : first + size] for ref in whole_refs]
        mine, came = (ref[rows_cut, start : start + size] for ref in (mine_ref, came_ref))
        left = jnp.concatenate(pieces + [jnp.where(lane == half, mine, came)], axis=0)
        return left if part else gelu(left.astype(jnp.float32)).astype(jnp.bfloat16)

    right = [right_refs[index][start : start + rows, :] for index, start in places]
    for k in range(1, groups - 1, 2):
        right[k], right[k + 1] = (
            jnp.where(lane == 0, right[k], right[k + 1]),
            jnp.where(lane == 0, right[k + 1], right[k]),
        )
    write_products(left_of, jnp.concatenate(right, axis=0), factor, out_ref, held, sems)


def products(part, factor, features, rights, order):
    rows = features[0].shape[0] // 2
    in_cols, columns = features[0].shape[1], rights[0].shape[1]
    spots = [(i, first) for i, right in enumerate(rights) for first in range(0, right.shape[0], rows)]
    places = [spots[order.index(k)] for k in range(len(order))]
    size = 128 if in_cols % 256 == 0 else in_cols // 2
    out = shape((in_cols, columns), jnp.float32)
    (result,) = call(
        functools.partial(block_products, part, factor, places), [out], (*features, *rights),
        2 * len(order) * rows * in_cols * columns, out_specs=[HBM],
        scratch=[pltpu.VMEM((in_cols // size, size, columns), jnp.float32), pltpu.SemaphoreType.DMA((in_cols // size,))],
        limit=(6 << 20) + 4 * in_cols * columns,
    )
    return result


def body(row_grads, row_dest, merger_in, hidden_pre, w_second):
    slots = row_grads[0]
    slot_count = slots.shape[0]
    before, inputs = hidden_pre[0], merger_in[0]
    merged_count, width = before.shape
    shards = lax.axis_size("roll")
    groups = lax.axis_size("enc")
    halves = shards // 2
    columns = slots.shape[1] // shards
    unit_cols = width // shards
    in_cols = width // groups
    kind = jnp.bfloat16
    aligned = in_cols % 256 == 0 and unit_cols % 128 == 0

    def spread(kept, came):
        blocks = call(pair_sum, [shape(kept.shape[1:], kind)] * halves, (kept, came), kept.size)
        return [blocks[0]] + [exchange(blocks[j], "roll", 2 * j) for j in range(1, halves)]

    place = (halves, merged_count, columns)
    outs = [shape(place, kind)] * 2
    if aligned:
        outs += [shape((2 * merged_count, in_cols), kind)] * (groups // 2)
        outs += [shape((2 * merged_count, in_cols // 2), kind), shape((merged_count, unit_cols), jnp.float32)]
    sources = [pltpu.with_memory_space_constraint(x, pltpu.HBM) for x in (row_dest, slots, before, inputs)]
    scratch = [
        pltpu.VMEM(row_dest.shape, row_dest.dtype),
        pltpu.VMEM(slots.shape, kind),
        pltpu.VMEM((merged_count, unit_cols), kind),
        pltpu.SemaphoreType.DMA((4 + 2 * halves + groups,)),
    ]
    kept, sent, *rest = call(
        functools.partial(front, halves, groups, int(aligned)), outs, sources,
        2 * slot_count * slots.size, in_specs=[HBM] * 4, scratch=scratch, limit=12 << 20,
    )
    if aligned:
        *blocks, slope = rest
    else:
        both = jnp.concatenate([before, inputs], axis=0)
        group = lax.axis_index("enc")
        blocks = []
        for distance, half in feature_cuts(groups):
            size = in_cols if half is None else in_cols // 2
            first = (group ^ distance) * in_cols + (0 if half is None else half * size)
            blocks.append(lax.dynamic_slice_in_dim(both, first, size, 1))
        own = lax.dynamic_slice_in_dim(before, lax.axis_index("roll") * unit_cols, unit_cols, 1)
        slope = gelu_slope(own.astype(jnp.float32))

    features = [blocks[0]]
    for block, k in zip(blocks[1:], range(1, groups, 2)):
        last = k == groups - 1
        pairs = [
            (e * shards + r, (e ^ (k if last else k + r % 2)) * shards + r) for e in range(groups) for r in range(shards)
        ]
        came = lax.ppermute(block, ("enc", "roll"), pairs)
        features += [came, exchange(came, "roll", 1)]

    pieces = spread(kept, exchange(sent, "roll", 1))
    (weights,) = call(
        load, [shape(w_second.shape, kind)], (pltpu.with_memory_space_constraint(w_second, pltpu.HBM),),
        in_specs=[HBM], scratch=[pltpu.SemaphoreType.DMA((8,))],
    )

    unit_shape = (halves, merged_count, unit_cols)
    flops = 2 * columns * math.prod(unit_shape)
    merged, sent = call(
        first_units, [shape((merged_count, columns), kind), shape(unit_shape, kind)], (*pieces, weights), flops,
    )
    came = exchange(sent, "roll", 1)
    (kept,) = call(second_units, [shape(unit_shape, kind)], (merged, weights), flops)

    merged_all, order, step = [merged], [0], groups // 2
    while step:
        (whole,) = (
            merged_all if len(order) == 1 else call(join, [shape((len(order) * merged_count, columns), kind)], merged_all)
        )
        merged_all = [whole, exchange(whole, "enc", step)]
        order += [k ^ step for k in order]
        step //= 2

    pieces = spread(kept, came)
    grads = (sum(piece.astype(jnp.float32) for piece in pieces) * slope).astype(kind)
    grads_all = [grads] + [exchange(grads, "enc", k) for k in range(1, groups)]

    factor = 1.0 / math.sqrt(merged_count * groups)
    grad_second = products(0, factor, features, merged_all, order)
    grad_first = products(1, factor, features, grads_all, list(range(groups)))
    return (grads[None], grad_first, grad_second)


def solution(mesh):
    return jax.shard_map(
        body,
        mesh=mesh,
        in_specs=(
            P("enc", "roll", None),
            P("enc", "roll"),
            P("enc", None, None),
            P("enc", None, None),
            P(None, "roll"),
        ),
        out_specs=(P("enc", None, "roll"), P("enc", "roll"), P("enc", "roll")),
        check_vma=False,
    )
```

```python
import functools
import math

import jax
import jax.numpy as jnp
from jax import lax
from jax.experimental import pallas as pl
from jax.experimental.pallas import tpu as pltpu
from jax.sharding import PartitionSpec as P


inv_root_two = 1.0 / math.sqrt(2.0)
inv_root_two_pi = 1.0 / math.sqrt(2.0 * math.pi)
VMEM = pl.BlockSpec(memory_space=pltpu.VMEM)
HBM = pl.BlockSpec(memory_space=pltpu.HBM)
shape = jax.ShapeDtypeStruct


def gelu_slope(values):
    return (
        0.5 * (1.0 + lax.erf(values * inv_root_two))
        + values * jnp.exp(-0.5 * values * values) * inv_root_two_pi
    )


def gelu(values):
    return 0.5 * values * (1.0 + lax.erf(values * inv_root_two))


def call(kernel, outs, args, flops=0, in_specs=None, out_specs=None, scratch=(), limit=4 << 20):
    moved = sum(math.prod(a.shape) * a.dtype.itemsize for a in list(outs) + list(args))
    return pl.pallas_call(
        kernel,
        out_shape=outs,
        in_specs=in_specs or [VMEM] * len(args),
        out_specs=out_specs or [VMEM] * len(outs),
        scratch_shapes=scratch,
        cost_estimate=pl.CostEstimate(flops=flops, bytes_accessed=moved, transcendentals=0),
        compiler_params=pltpu.CompilerParams(vmem_limit_bytes=limit),
    )(*args)


def exchange(block, axis, step):
    pairs = [(i, i ^ step) for i in range(lax.axis_size(axis))]
    return lax.ppermute(block, axis, pairs)


def feature_cuts(groups):
    lane = lax.axis_index("roll") % 2
    return [(0, None)] + [(k + lane, None) for k in range(1, groups - 1, 2)] + [(groups - 1, lane)]


def front(halves, groups, aligned, *refs):
    dest_ref, slots_ref, before_ref, inputs_ref = refs[:4]
    placed_refs, rest = refs[4:6], refs[6:]
    count = groups // 2 + 1
    feature_refs = rest[: count * aligned]
    held_dest, held, sems = rest[count * aligned :]
    _, merged_count, columns = placed_refs[0].shape
    shard, group = lax.axis_index("roll"), lax.axis_index("enc")
    started = iter(range(sems.shape[0]))

    def fetch(source, target):
        copy = pltpu.make_async_copy(source, target, sems.at[next(started)])
        copy.start()
        return copy

    def cut(index, size):
        return pl.ds(pl.multiple_of(index * size, size), size)

    dest_copy = fetch(dest_ref, held_dest)
    spots = [2 * j + parity for parity in (1, 0) for j in range(halves)]
    slot_copies = [
        fetch(slots_ref.at[:, cut(shard ^ k, columns)], held.at[:, pl.ds(i * columns, columns)]) for i, k in enumerate(spots)
    ]
    before_copies, input_copies = [], []
    for ref, (distance, half) in zip(feature_refs, feature_cuts(groups)):
        index = group ^ distance
        source = cut(index if half is None else 2 * index + half, ref.shape[1])
        before_copies.append(fetch(before_ref.at[:, source], ref.at[pl.ds(0, merged_count), :]))
        input_copies.append(fetch(inputs_ref.at[:, source], ref.at[pl.ds(merged_count, merged_count), :]))
    dest_copy.wait()
    rows = lax.broadcasted_iota(jnp.int32, (merged_count, held.shape[0]), 0)
    picker = jnp.where(rows == held_dest[...], 1.0, 0.0).astype(jnp.bfloat16)
    for copy in slot_copies:
        copy.wait()
    placed = jnp.dot(picker, held[...], preferred_element_type=jnp.float32).astype(jnp.bfloat16)
    for i, k in enumerate(spots):
        placed_refs[k % 2][k // 2] = placed[:, i * columns : (i + 1) * columns]
    for copy in before_copies + input_copies:
        copy.wait()


def join(*refs):
    *piece_refs, out_ref = refs
    first = 0
    for ref in piece_refs:
        out_ref[first : first + ref.shape[0], :] = ref[...]
        first += ref.shape[0]


def own_slope(before_ref, out_ref, held, sem):
    size = out_ref.shape[1]
    first = pl.multiple_of(lax.axis_index("roll") * size, size)
    copy = pltpu.make_async_copy(before_ref.at[:, pl.ds(first, size)], held, sem)
    copy.start()
    copy.wait()
    out_ref[...] = gelu_slope(held[...].astype(jnp.float32))


def pair_sum(kept_ref, came_ref, *out_refs):
    for j, out_ref in enumerate(out_refs):
        out_ref[...] = (kept_ref[j].astype(jnp.float32) + came_ref[j].astype(jnp.float32)).astype(jnp.bfloat16)


def unit_blocks(parity, merged, w_ref, out_ref):
    shard = lax.axis_index("roll")
    halves, _, unit_cols = out_ref.shape
    for j in range(halves):
        first = pl.multiple_of((shard ^ (2 * j + parity)) * unit_cols, unit_cols)
        out_ref[j] = lax.dot_general(
            merged, w_ref[pl.ds(first, unit_cols), :], (((1,), (1,)), ((), ())), preferred_element_type=jnp.float32
        ).astype(jnp.bfloat16)


def first_units(*refs):
    *piece_refs, w_ref, merged_ref, out_ref = refs
    total = piece_refs[0][...].astype(jnp.float32)
    for piece_ref in piece_refs[1:]:
        total = total + piece_ref[...].astype(jnp.float32)
    merged_ref[...] = total.astype(jnp.bfloat16)
    unit_blocks(1, merged_ref[...], w_ref, out_ref)


def second_units(merged_ref, w_ref, out_ref):
    unit_blocks(0, merged_ref[...], w_ref, out_ref)


def write_products(left_of, right, factor, out_ref, held, sems):
    size = held.shape[1]
    copies = []
    for j in range(held.shape[0]):
        held[j] = lax.dot_general(
            left_of(j * size, size), right, (((0,), (0,)), ((), ())), preferred_element_type=jnp.float32
        ) * factor
        copies.append(pltpu.make_async_copy(held.at[j], out_ref.at[pl.ds(j * size, size), :], sems.at[j]))
        copies[-1].start()
    for copy in copies:
        copy.wait()


def block_products(part, factor, places, *refs):
    groups = len(places)
    feature_refs, right_refs, (out_ref, held, sems) = refs[: groups + 1], refs[groups + 1 : -3], refs[-3:]
    *whole_refs, mine_ref, came_ref = feature_refs
    rows = mine_ref.shape[0] // 2
    rows_cut = slice(part * rows, (part + 1) * rows)
    half_cols = mine_ref.shape[1]
    lane = lax.axis_index("roll") % 2

    def left_of(first, size):
        half, start = divmod(first, half_cols)
        pieces = [ref[rows_cut, first : first + size] for ref in whole_refs]
        mine, came = (ref[rows_cut, start : start + size] for ref in (mine_ref, came_ref))
        left = jnp.concatenate(pieces + [jnp.where(lane == half, mine, came)], axis=0)
        return left if part else gelu(left.astype(jnp.float32)).astype(jnp.bfloat16)

    right = [right_refs[index][start : start + rows, :] for index, start in places]
    for k in range(1, groups - 1, 2):
        right[k], right[k + 1] = (
            jnp.where(lane == 0, right[k], right[k + 1]),
            jnp.where(lane == 0, right[k + 1], right[k]),
        )
    write_products(left_of, jnp.concatenate(right, axis=0), factor, out_ref, held, sems)


def products(part, factor, features, rights, order):
    rows = features[0].shape[0] // 2
    in_cols, columns = features[0].shape[1], rights[0].shape[1]
    spots = [(i, first) for i, right in enumerate(rights) for first in range(0, right.shape[0], rows)]
    places = [spots[order.index(k)] for k in range(len(order))]
    size = 128 if in_cols % 256 == 0 else in_cols // 2
    out = shape((in_cols, columns), jnp.float32)
    (result,) = call(
        functools.partial(block_products, part, factor, places), [out], (*features, *rights),
        2 * len(order) * rows * in_cols * columns, out_specs=[HBM],
        scratch=[pltpu.VMEM((in_cols // size, size, columns), jnp.float32), pltpu.SemaphoreType.DMA((in_cols // size,))],
        limit=(6 << 20) + 4 * in_cols * columns,
    )
    return result


def body(row_grads, row_dest, merger_in, hidden_pre, w_second):
    slots = row_grads[0]
    slot_count = slots.shape[0]
    before, inputs = hidden_pre[0], merger_in[0]
    merged_count, width = before.shape
    shards = lax.axis_size("roll")
    groups = lax.axis_size("enc")
    halves = shards // 2
    columns = slots.shape[1] // shards
    unit_cols = width // shards
    in_cols = width // groups
    kind = jnp.bfloat16
    aligned = in_cols % 256 == 0 and unit_cols % 128 == 0

    def spread(kept, came):
        blocks = call(pair_sum, [shape(kept.shape[1:], kind)] * halves, (kept, came), 20_000_000_000)
        return [blocks[0]] + [exchange(blocks[j], "roll", 2 * j) for j in range(1, halves)]

    place = (halves, merged_count, columns)
    outs = [shape(place, kind)] * 2
    if aligned:
        outs += [shape((2 * merged_count, in_cols), kind)] * (groups // 2)
        outs += [shape((2 * merged_count, in_cols // 2), kind)]
    sources = [pltpu.with_memory_space_constraint(x, pltpu.HBM) for x in (row_dest, slots, before, inputs)]
    scratch = [
        pltpu.VMEM(row_dest.shape, row_dest.dtype),
        pltpu.VMEM(slots.shape, kind),
        pltpu.SemaphoreType.DMA((3 + 2 * halves + groups,)),
    ]
    kept, sent, *rest = call(
        functools.partial(front, halves, groups, int(aligned)), outs, sources,
        2 * slot_count * slots.size, in_specs=[HBM] * 4, scratch=scratch, limit=12 << 20,
    )
    if aligned:
        blocks = rest
        (slope,) = call(
            own_slope, [shape((merged_count, unit_cols), jnp.float32)], (sources[2],), in_specs=[HBM],
            scratch=[pltpu.VMEM((merged_count, unit_cols), kind), pltpu.SemaphoreType.DMA],
        )
    else:
        both = jnp.concatenate([before, inputs], axis=0)
        group = lax.axis_index("enc")
        blocks = []
        for distance, half in feature_cuts(groups):
            size = in_cols if half is None else in_cols // 2
            first = (group ^ distance) * in_cols + (0 if half is None else half * size)
            blocks.append(lax.dynamic_slice_in_dim(both, first, size, 1))
        own = lax.dynamic_slice_in_dim(before, lax.axis_index("roll") * unit_cols, unit_cols, 1)
        slope = gelu_slope(own.astype(jnp.float32))

    features = [blocks[0]]
    for block, k in zip(blocks[1:], range(1, groups, 2)):
        last = k == groups - 1
        pairs = [
            (e * shards + r, (e ^ (k if last else k + r % 2)) * shards + r) for e in range(groups) for r in range(shards)
        ]
        came = lax.ppermute(block, ("enc", "roll"), pairs)
        features += [came, exchange(came, "roll", 1)]

    pieces = spread(kept, exchange(sent, "roll", 1))
    weights = w_second

    unit_shape = (halves, merged_count, unit_cols)
    flops = 2 * columns * math.prod(unit_shape)
    merged, sent = call(
        first_units, [shape((merged_count, columns), kind), shape(unit_shape, kind)], (*pieces, weights), flops,
    )
    came = exchange(sent, "roll", 1)
    (kept,) = call(second_units, [shape(unit_shape, kind)], (merged, weights), flops)

    merged_all, order, step = [merged], [0], groups // 2
    while step:
        (whole,) = (
            merged_all if len(order) == 1 else call(join, [shape((len(order) * merged_count, columns), kind)], merged_all)
        )
        merged_all = [whole, exchange(whole, "enc", step)]
        order += [k ^ step for k in order]
        step //= 2

    pieces = spread(kept, came)
    grads = (sum(piece.astype(jnp.float32) for piece in pieces) * slope).astype(kind)
    grads_all = [grads] + [exchange(grads, "enc", k) for k in range(1, groups)]

    factor = 1.0 / math.sqrt(merged_count * groups)
    grad_second = products(0, factor, features, merged_all, order)
    grad_first = products(1, factor, features, grads_all, list(range(groups)))
    return (grads[None], grad_first, grad_second)


def solution(mesh):
    return jax.shard_map(
        body,
        mesh=mesh,
        in_specs=(
            P("enc", "roll", None),
            P("enc", "roll"),
            P("enc", None, None),
            P("enc", None, None),
            P(None, "roll"),
        ),
        out_specs=(P("enc", None, "roll"), P("enc", "roll"), P("enc", "roll")),
        check_vma=False,
    )
```

```python
import functools
import math

import jax
import jax.numpy as jnp
from jax import lax
from jax.experimental import pallas as pl
from jax.experimental.pallas import tpu as pltpu
from jax.sharding import PartitionSpec as P


inv_root_two = 1.0 / math.sqrt(2.0)
inv_root_two_pi = 1.0 / math.sqrt(2.0 * math.pi)
VMEM = pl.BlockSpec(memory_space=pltpu.VMEM)
HBM = pl.BlockSpec(memory_space=pltpu.HBM)
shape = jax.ShapeDtypeStruct


def gelu_slope(values):
    return (
        0.5 * (1.0 + lax.erf(values * inv_root_two))
        + values * jnp.exp(-0.5 * values * values) * inv_root_two_pi
    )


def gelu(values):
    return 0.5 * values * (1.0 + lax.erf(values * inv_root_two))


def call(kernel, outs, args, flops=0, in_specs=None, out_specs=None, scratch=(), limit=4 << 20):
    moved = sum(math.prod(a.shape) * a.dtype.itemsize for a in list(outs) + list(args))
    return pl.pallas_call(
        kernel,
        out_shape=outs,
        in_specs=in_specs or [VMEM] * len(args),
        out_specs=out_specs or [VMEM] * len(outs),
        scratch_shapes=scratch,
        cost_estimate=pl.CostEstimate(flops=flops, bytes_accessed=moved, transcendentals=0),
        compiler_params=pltpu.CompilerParams(vmem_limit_bytes=limit),
    )(*args)


def exchange(block, axis, step):
    pairs = [(i, i ^ step) for i in range(lax.axis_size(axis))]
    return lax.ppermute(block, axis, pairs)


def feature_cuts(groups):
    lane = lax.axis_index("roll") % 2
    return [(0, None)] + [(k + lane, None) for k in range(1, groups - 1, 2)] + [(groups - 1, lane)]


def front(halves, groups, aligned, *refs):
    dest_ref, slots_ref, before_ref, inputs_ref = refs[:4]
    placed_refs, rest = refs[4:6], refs[6:]
    count = groups // 2 + 1
    feature_refs = rest[: count * aligned]
    held_dest, held, sems = rest[count * aligned :]
    _, merged_count, columns = placed_refs[0].shape
    shard, group = lax.axis_index("roll"), lax.axis_index("enc")
    started = iter(range(sems.shape[0]))

    def fetch(source, target):
        copy = pltpu.make_async_copy(source, target, sems.at[next(started)])
        copy.start()
        return copy

    def cut(index, size):
        return pl.ds(pl.multiple_of(index * size, size), size)

    dest_copy = fetch(dest_ref, held_dest)
    spots = [2 * j + parity for parity in (1, 0) for j in range(halves)]
    slot_copies = [
        fetch(slots_ref.at[:, cut(shard ^ k, columns)], held.at[:, pl.ds(i * columns, columns)]) for i, k in enumerate(spots)
    ]
    before_copies, input_copies = [], []
    for ref, (distance, half) in zip(feature_refs, feature_cuts(groups)):
        index = group ^ distance
        source = cut(index if half is None else 2 * index + half, ref.shape[1])
        before_copies.append(fetch(before_ref.at[:, source], ref.at[pl.ds(0, merged_count), :]))
        input_copies.append(fetch(inputs_ref.at[:, source], ref.at[pl.ds(merged_count, merged_count), :]))
    dest_copy.wait()
    rows = lax.broadcasted_iota(jnp.int32, (merged_count, held.shape[0]), 0)
    picker = jnp.where(rows == held_dest[...], 1.0, 0.0).astype(jnp.bfloat16)
    for copy in slot_copies:
        copy.wait()
    placed = jnp.dot(picker, held[...], preferred_element_type=jnp.float32).astype(jnp.bfloat16)
    for i, k in enumerate(spots):
        placed_refs[k % 2][k // 2] = placed[:, i * columns : (i + 1) * columns]
    for copy in before_copies + input_copies:
        copy.wait()


def join(*refs):
    *piece_refs, out_ref = refs
    first = 0
    for ref in piece_refs:
        out_ref[first : first + ref.shape[0], :] = ref[...]
        first += ref.shape[0]


def own_slope(before_ref, out_ref, held, sem):
    size = out_ref.shape[1]
    first = pl.multiple_of(lax.axis_index("roll") * size, size)
    copy = pltpu.make_async_copy(before_ref.at[:, pl.ds(first, size)], held, sem)
    copy.start()
    copy.wait()
    out_ref[...] = gelu_slope(held[...].astype(jnp.float32))


def pair_sum(kept_ref, came_ref, *out_refs):
    for j, out_ref in enumerate(out_refs):
        out_ref[...] = (kept_ref[j].astype(jnp.float32) + came_ref[j].astype(jnp.float32)).astype(jnp.bfloat16)


def unit_blocks(parity, merged, w_ref, out_ref):
    shard = lax.axis_index("roll")
    halves, _, unit_cols = out_ref.shape
    turned = merged.T
    for j in range(halves):
        first = pl.multiple_of((shard ^ (2 * j + parity)) * unit_cols, unit_cols)
        out_ref[j] = lax.dot_general(
            w_ref[pl.ds(first, unit_cols), :], turned, (((1,), (0,)), ((), ())), preferred_element_type=jnp.float32
        ).T.astype(jnp.bfloat16)


def first_units(*refs):
    *piece_refs, w_ref, merged_ref, out_ref = refs
    total = piece_refs[0][...].astype(jnp.float32)
    for piece_ref in piece_refs[1:]:
        total = total + piece_ref[...].astype(jnp.float32)
    merged_ref[...] = total.astype(jnp.bfloat16)
    unit_blocks(1, merged_ref[...], w_ref, out_ref)


def second_units(merged_ref, w_ref, out_ref):
    unit_blocks(0, merged_ref[...], w_ref, out_ref)


def write_products(left_of, right, left_dim, factor, out_ref, held, sems):
    size = held.shape[1]
    copies = []
    for j in range(held.shape[0]):
        held[j] = lax.dot_general(
            left_of(j * size, size), right, (((left_dim,), (0,)), ((), ())), preferred_element_type=jnp.float32
        ) * factor
        copies.append(pltpu.make_async_copy(held.at[j], out_ref.at[pl.ds(j * size, size), :], sems.at[j]))
        copies[-1].start()
    for copy in copies:
        copy.wait()


def right_blocks(places, rows, refs):
    groups = len(places)
    lane = lax.axis_index("roll") % 2
    right = [refs[index][start : start + rows, :] for index, start in places]
    for k in range(1, groups - 1, 2):
        right[k], right[k + 1] = (
            jnp.where(lane == 0, right[k], right[k + 1]),
            jnp.where(lane == 0, right[k + 1], right[k]),
        )
    return jnp.concatenate(right, axis=0)


def second_products(factor, places, *refs):
    groups = len(places)
    feature_refs, right_refs, (out_ref, turned_ref, held, sems) = refs[: groups + 1], refs[groups + 1 : -4], refs[-4:]
    *whole_refs, mine_ref, came_ref = feature_refs
    rows, half_cols = mine_ref.shape[0] // 2, mine_ref.shape[1]
    lane = lax.axis_index("roll") % 2

    def features_of(part, first, size):
        rows_cut = slice(part * rows, (part + 1) * rows)
        half, start = divmod(first, half_cols)
        pieces = [ref[rows_cut, first : first + size] for ref in whole_refs]
        mine, came = (ref[rows_cut, start : start + size] for ref in (mine_ref, came_ref))
        return jnp.concatenate(pieces + [jnp.where(lane == half, mine, came)], axis=0)

    def left_of(first, size):
        turned_ref[first : first + size, :] = features_of(1, first, size).T
        return gelu(features_of(0, first, size).astype(jnp.float32)).astype(jnp.bfloat16)

    write_products(left_of, right_blocks(places, rows, right_refs), 0, factor, out_ref, held, sems)


def first_products(factor, places, turned_ref, *refs):
    right_refs, (out_ref, held, sems) = refs[:-3], refs[-3:]
    rows = turned_ref.shape[1] // len(places)

    def left_of(first, size):
        return turned_ref[first : first + size, :]

    write_products(left_of, right_blocks(places, rows, right_refs), 1, factor, out_ref, held, sems)


def products(kernel, factor, lefts, rights, order, in_cols, rows, extra):
    columns = rights[0].shape[1]
    spots = [(i, first) for i, right in enumerate(rights) for first in range(0, right.shape[0], rows)]
    places = [spots[order.index(k)] for k in range(len(order))]
    size = 128 if in_cols % 256 == 0 else in_cols // 2
    out = shape((in_cols, columns), jnp.float32)
    return call(
        functools.partial(kernel, factor, places), [out, *extra], (*lefts, *rights),
        2 * len(order) * rows * in_cols * columns, out_specs=[HBM] + [VMEM] * len(extra),
        scratch=[pltpu.VMEM((in_cols // size, size, columns), jnp.float32), pltpu.SemaphoreType.DMA((in_cols // size,))],
        limit=(6 << 20) + 4 * in_cols * columns,
    )


def body(row_grads, row_dest, merger_in, hidden_pre, w_second):
    slots = row_grads[0]
    slot_count = slots.shape[0]
    before, inputs = hidden_pre[0], merger_in[0]
    merged_count, width = before.shape
    shards = lax.axis_size("roll")
    groups = lax.axis_size("enc")
    halves = shards // 2
    columns = slots.shape[1] // shards
    unit_cols = width // shards
    in_cols = width // groups
    kind = jnp.bfloat16
    aligned = in_cols % 256 == 0 and unit_cols % 128 == 0

    def spread(kept, came):
        blocks = call(pair_sum, [shape(kept.shape[1:], kind)] * halves, (kept, came), 20_000_000_000)
        return [blocks[0]] + [exchange(blocks[j], "roll", 2 * j) for j in range(1, halves)]

    place = (halves, merged_count, columns)
    outs = [shape(place, kind)] * 2
    if aligned:
        outs += [shape((2 * merged_count, in_cols), kind)] * (groups // 2)
        outs += [shape((2 * merged_count, in_cols // 2), kind)]
    sources = [pltpu.with_memory_space_constraint(x, pltpu.HBM) for x in (row_dest, slots, before, inputs)]
    scratch = [
        pltpu.VMEM(row_dest.shape, row_dest.dtype),
        pltpu.VMEM(slots.shape, kind),
        pltpu.SemaphoreType.DMA((3 + 2 * halves + groups,)),
    ]
    kept, sent, *rest = call(
        functools.partial(front, halves, groups, int(aligned)), outs, sources,
        2 * slot_count * slots.size, in_specs=[HBM] * 4, scratch=scratch, limit=12 << 20,
    )
    if aligned:
        blocks = rest
        (slope,) = call(
            own_slope, [shape((merged_count, unit_cols), jnp.float32)], (sources[2],), in_specs=[HBM],
            scratch=[pltpu.VMEM((merged_count, unit_cols), kind), pltpu.SemaphoreType.DMA],
        )
    else:
        both = jnp.concatenate([before, inputs], axis=0)
        group = lax.axis_index("enc")
        blocks = []
        for distance, half in feature_cuts(groups):
            size = in_cols if half is None else in_cols // 2
            first = (group ^ distance) * in_cols + (0 if half is None else half * size)
            blocks.append(lax.dynamic_slice_in_dim(both, first, size, 1))
        own = lax.dynamic_slice_in_dim(before, lax.axis_index("roll") * unit_cols, unit_cols, 1)
        slope = gelu_slope(own.astype(jnp.float32))

    features = [blocks[0]]
    for block, k in zip(blocks[1:], range(1, groups, 2)):
        last = k == groups - 1
        pairs = [
            (e * shards + r, (e ^ (k if last else k + r % 2)) * shards + r) for e in range(groups) for r in range(shards)
        ]
        came = lax.ppermute(block, ("enc", "roll"), pairs)
        features += [came, exchange(came, "roll", 1)]

    pieces = spread(kept, exchange(sent, "roll", 1))
    unit_shape = (halves, merged_count, unit_cols)
    flops = 2 * columns * math.prod(unit_shape)
    merged, sent = call(
        first_units, [shape((merged_count, columns), kind), shape(unit_shape, kind)], (*pieces, w_second), flops,
    )
    came = exchange(sent, "roll", 1)
    (kept,) = call(second_units, [shape(unit_shape, kind)], (merged, w_second), flops)

    merged_all, order, step = [merged], [0], groups // 2
    while step:
        (whole,) = (
            merged_all if len(order) == 1 else call(join, [shape((len(order) * merged_count, columns), kind)], merged_all)
        )
        merged_all = [whole, exchange(whole, "enc", step)]
        order += [k ^ step for k in order]
        step //= 2

    pieces = spread(kept, came)
    grads = (sum(piece.astype(jnp.float32) for piece in pieces) * slope).astype(kind)
    grads_all = [grads] + [exchange(grads, "enc", k) for k in range(1, groups)]

    factor = 1.0 / math.sqrt(merged_count * groups)
    turned = shape((in_cols, groups * merged_count), kind)
    grad_second, turned = products(
        second_products, factor, features, merged_all, order, in_cols, merged_count, [turned]
    )
    (grad_first,) = products(
        first_products, factor, [turned], grads_all, list(range(groups)), in_cols, merged_count, []
    )
    return (grads[None], grad_first, grad_second)


def solution(mesh):
    return jax.shard_map(
        body,
        mesh=mesh,
        in_specs=(
            P("enc", "roll", None),
            P("enc", "roll"),
            P("enc", None, None),
            P("enc", None, None),
            P(None, "roll"),
        ),
        out_specs=(P("enc", None, "roll"), P("enc", "roll"), P("enc", "roll")),
        check_vma=False,
    )
```

```python
import functools
import math

import jax
import jax.numpy as jnp
from jax import lax
from jax.experimental import pallas as pl
from jax.experimental.pallas import tpu as pltpu
from jax.sharding import PartitionSpec as P


inv_root_two = 1.0 / math.sqrt(2.0)
inv_root_two_pi = 1.0 / math.sqrt(2.0 * math.pi)
VMEM = pl.BlockSpec(memory_space=pltpu.VMEM)
HBM = pl.BlockSpec(memory_space=pltpu.HBM)
shape = jax.ShapeDtypeStruct


def gelu_slope(values):
    return (
        0.5 * (1.0 + lax.erf(values * inv_root_two))
        + values * jnp.exp(-0.5 * values * values) * inv_root_two_pi
    )


def gelu(values):
    return 0.5 * values * (1.0 + lax.erf(values * inv_root_two))


def call(kernel, outs, args, flops=0, in_specs=None, out_specs=None, scratch=(), limit=4 << 20):
    moved = sum(math.prod(a.shape) * a.dtype.itemsize for a in list(outs) + list(args))
    return pl.pallas_call(
        kernel,
        out_shape=outs,
        in_specs=in_specs or [VMEM] * len(args),
        out_specs=out_specs or [VMEM] * len(outs),
        scratch_shapes=scratch,
        cost_estimate=pl.CostEstimate(flops=flops, bytes_accessed=moved, transcendentals=0),
        compiler_params=pltpu.CompilerParams(vmem_limit_bytes=limit),
    )(*args)


def exchange(block, axis, step):
    pairs = [(i, i ^ step) for i in range(lax.axis_size(axis))]
    return lax.ppermute(block, axis, pairs)


def feature_cuts(groups):
    lane = lax.axis_index("roll") % 2
    return [(0, None)] + [(k + lane, None) for k in range(1, groups - 1, 2)] + [(groups - 1, lane)]


def front(halves, groups, aligned, *refs):
    dest_ref, slots_ref, before_ref, inputs_ref = refs[:4]
    placed_refs, rest = refs[4:6], refs[6:]
    count = groups // 2 + 1
    feature_refs = rest[: count * aligned]
    held_dest, held, sems = rest[count * aligned :]
    _, merged_count, columns = placed_refs[0].shape
    shard, group = lax.axis_index("roll"), lax.axis_index("enc")
    started = iter(range(sems.shape[0]))

    def fetch(source, target):
        copy = pltpu.make_async_copy(source, target, sems.at[next(started)])
        copy.start()
        return copy

    def cut(index, size):
        return pl.ds(pl.multiple_of(index * size, size), size)

    dest_copy = fetch(dest_ref, held_dest)
    spots = [2 * j + parity for parity in (1, 0) for j in range(halves)]
    slot_copies = [
        fetch(slots_ref.at[:, cut(shard ^ k, columns)], held.at[:, pl.ds(i * columns, columns)]) for i, k in enumerate(spots)
    ]
    before_copies, input_copies = [], []
    for ref, (distance, half) in zip(feature_refs, feature_cuts(groups)):
        index = group ^ distance
        source = cut(index if half is None else 2 * index + half, ref.shape[1])
        before_copies.append(fetch(before_ref.at[:, source], ref.at[pl.ds(0, merged_count), :]))
        input_copies.append(fetch(inputs_ref.at[:, source], ref.at[pl.ds(merged_count, merged_count), :]))
    dest_copy.wait()
    rows = lax.broadcasted_iota(jnp.int32, (merged_count, held.shape[0]), 0)
    picker = jnp.where(rows == held_dest[...], 1.0, 0.0).astype(jnp.bfloat16)
    for copy in slot_copies:
        copy.wait()
    placed = jnp.dot(picker, held[...], preferred_element_type=jnp.float32).astype(jnp.bfloat16)
    for i, k in enumerate(spots):
        placed_refs[k % 2][k // 2] = placed[:, i * columns : (i + 1) * columns]
    for copy in before_copies + input_copies:
        copy.wait()


def join(*refs):
    *piece_refs, out_ref = refs
    first = 0
    for ref in piece_refs:
        out_ref[first : first + ref.shape[0], :] = ref[...]
        first += ref.shape[0]


def own_slope(before_ref, out_ref, held, sem):
    size = out_ref.shape[1]
    first = pl.multiple_of(lax.axis_index("roll") * size, size)
    copy = pltpu.make_async_copy(before_ref.at[:, pl.ds(first, size)], held, sem)
    copy.start()
    copy.wait()
    out_ref[...] = gelu_slope(held[...].astype(jnp.float32))


def pair_sum(kept_ref, came_ref, *out_refs):
    for j, out_ref in enumerate(out_refs):
        out_ref[...] = (kept_ref[j].astype(jnp.float32) + came_ref[j].astype(jnp.float32)).astype(jnp.bfloat16)


def unit_blocks(parity, merged, w_ref, out_ref):
    shard = lax.axis_index("roll")
    halves, _, unit_cols = out_ref.shape
    turned = merged.T
    for j in range(halves):
        first = pl.multiple_of((shard ^ (2 * j + parity)) * unit_cols, unit_cols)
        rows = w_ref[pl.ds(first, unit_cols), :]
        if j % 2:
            out_ref[j] = lax.dot_general(
                merged, rows, (((1,), (1,)), ((), ())), preferred_element_type=jnp.float32
            ).astype(jnp.bfloat16)
        else:
            out_ref[j] = jnp.dot(rows, turned, preferred_element_type=jnp.float32).T.astype(jnp.bfloat16)


def first_units(*refs):
    *piece_refs, w_ref, merged_ref, out_ref = refs
    total = piece_refs[0][...].astype(jnp.float32)
    for piece_ref in piece_refs[1:]:
        total = total + piece_ref[...].astype(jnp.float32)
    merged_ref[...] = total.astype(jnp.bfloat16)
    unit_blocks(1, merged_ref[...], w_ref, out_ref)


def second_units(merged_ref, w_ref, out_ref):
    unit_blocks(0, merged_ref[...], w_ref, out_ref)


def write_products(left_of, right, left_dim, factor, out_ref, held, sems):
    size = held.shape[1]
    copies = []
    for j in range(held.shape[0]):
        held[j] = lax.dot_general(
            left_of(j * size, size), right, (((left_dim,), (0,)), ((), ())), preferred_element_type=jnp.float32
        ) * factor
        copies.append(pltpu.make_async_copy(held.at[j], out_ref.at[pl.ds(j * size, size), :], sems.at[j]))
        copies[-1].start()
    for copy in copies:
        copy.wait()


def right_blocks(places, rows, refs):
    groups = len(places)
    lane = lax.axis_index("roll") % 2
    right = [refs[index][start : start + rows, :] for index, start in places]
    for k in range(1, groups - 1, 2):
        right[k], right[k + 1] = (
            jnp.where(lane == 0, right[k], right[k + 1]),
            jnp.where(lane == 0, right[k + 1], right[k]),
        )
    return jnp.concatenate(right, axis=0)


def second_products(factor, places, *refs):
    groups = len(places)
    feature_refs, right_refs, (out_ref, turned_ref, held, sems) = refs[: groups + 1], refs[groups + 1 : -4], refs[-4:]
    *whole_refs, mine_ref, came_ref = feature_refs
    rows, half_cols = mine_ref.shape[0] // 2, mine_ref.shape[1]
    lane = lax.axis_index("roll") % 2

    def features_of(part, first, size):
        rows_cut = slice(part * rows, (part + 1) * rows)
        half, start = divmod(first, half_cols)
        pieces = [ref[rows_cut, first : first + size] for ref in whole_refs]
        mine, came = (ref[rows_cut, start : start + size] for ref in (mine_ref, came_ref))
        return jnp.concatenate(pieces + [jnp.where(lane == half, mine, came)], axis=0)

    def left_of(first, size):
        turned_ref[first : first + size, :] = features_of(1, first, size).T
        return gelu(features_of(0, first, size).astype(jnp.float32)).astype(jnp.bfloat16)

    write_products(left_of, right_blocks(places, rows, right_refs), 0, factor, out_ref, held, sems)


def first_products(factor, places, turned_ref, *refs):
    right_refs, (out_ref, held, sems) = refs[:-3], refs[-3:]
    rows = turned_ref.shape[1] // len(places)

    def left_of(first, size):
        return turned_ref[first : first + size, :]

    write_products(left_of, right_blocks(places, rows, right_refs), 1, factor, out_ref, held, sems)


def products(kernel, factor, lefts, rights, order, in_cols, rows, extra):
    columns = rights[0].shape[1]
    spots = [(i, first) for i, right in enumerate(rights) for first in range(0, right.shape[0], rows)]
    places = [spots[order.index(k)] for k in range(len(order))]
    size = 128 if in_cols % 256 == 0 else in_cols // 2
    out = shape((in_cols, columns), jnp.float32)
    return call(
        functools.partial(kernel, factor, places), [out, *extra], (*lefts, *rights),
        2 * len(order) * rows * in_cols * columns, out_specs=[HBM] + [VMEM] * len(extra),
        scratch=[pltpu.VMEM((in_cols // size, size, columns), jnp.float32), pltpu.SemaphoreType.DMA((in_cols // size,))],
        limit=(6 << 20) + 4 * in_cols * columns,
    )


def body(row_grads, row_dest, merger_in, hidden_pre, w_second):
    slots = row_grads[0]
    slot_count = slots.shape[0]
    before, inputs = hidden_pre[0], merger_in[0]
    merged_count, width = before.shape
    shards = lax.axis_size("roll")
    groups = lax.axis_size("enc")
    halves = shards // 2
    columns = slots.shape[1] // shards
    unit_cols = width // shards
    in_cols = width // groups
    kind = jnp.bfloat16
    aligned = in_cols % 256 == 0 and unit_cols % 128 == 0

    def spread(kept, came):
        blocks = call(pair_sum, [shape(kept.shape[1:], kind)] * halves, (kept, came), 20_000_000_000)
        return [blocks[0]] + [exchange(blocks[j], "roll", 2 * j) for j in range(1, halves)]

    place = (halves, merged_count, columns)
    outs = [shape(place, kind)] * 2
    if aligned:
        outs += [shape((2 * merged_count, in_cols), kind)] * (groups // 2)
        outs += [shape((2 * merged_count, in_cols // 2), kind)]
    sources = [pltpu.with_memory_space_constraint(x, pltpu.HBM) for x in (row_dest, slots, before, inputs)]
    scratch = [
        pltpu.VMEM(row_dest.shape, row_dest.dtype),
        pltpu.VMEM(slots.shape, kind),
        pltpu.SemaphoreType.DMA((3 + 2 * halves + groups,)),
    ]
    kept, sent, *rest = call(
        functools.partial(front, halves, groups, int(aligned)), outs, sources,
        2 * slot_count * slots.size, in_specs=[HBM] * 4, scratch=scratch, limit=12 << 20,
    )
    if aligned:
        blocks = rest
        (slope,) = call(
            own_slope, [shape((merged_count, unit_cols), jnp.float32)], (sources[2],), in_specs=[HBM],
            scratch=[pltpu.VMEM((merged_count, unit_cols), kind), pltpu.SemaphoreType.DMA],
        )
    else:
        both = jnp.concatenate([before, inputs], axis=0)
        group = lax.axis_index("enc")
        blocks = []
        for distance, half in feature_cuts(groups):
            size = in_cols if half is None else in_cols // 2
            first = (group ^ distance) * in_cols + (0 if half is None else half * size)
            blocks.append(lax.dynamic_slice_in_dim(both, first, size, 1))
        own = lax.dynamic_slice_in_dim(before, lax.axis_index("roll") * unit_cols, unit_cols, 1)
        slope = gelu_slope(own.astype(jnp.float32))

    features = [blocks[0]]
    for block, k in zip(blocks[1:], range(1, groups, 2)):
        last = k == groups - 1
        pairs = [
            (e * shards + r, (e ^ (k if last else k + r % 2)) * shards + r) for e in range(groups) for r in range(shards)
        ]
        came = lax.ppermute(block, ("enc", "roll"), pairs)
        features += [came, exchange(came, "roll", 1)]

    pieces = spread(kept, exchange(sent, "roll", 1))
    unit_shape = (halves, merged_count, unit_cols)
    flops = 2 * columns * math.prod(unit_shape)
    merged, sent = call(
        first_units, [shape((merged_count, columns), kind), shape(unit_shape, kind)], (*pieces, w_second), flops,
    )
    came = exchange(sent, "roll", 1)
    (kept,) = call(second_units, [shape(unit_shape, kind)], (merged, w_second), flops)

    merged_all, order, step = [merged], [0], groups // 2
    while step:
        (whole,) = (
            merged_all if len(order) == 1 else call(join, [shape((len(order) * merged_count, columns), kind)], merged_all)
        )
        merged_all = [whole, exchange(whole, "enc", step)]
        order += [k ^ step for k in order]
        step //= 2

    pieces = spread(kept, came)
    grads = (sum(piece.astype(jnp.float32) for piece in pieces) * slope).astype(kind)
    grads_all = [grads] + [exchange(grads, "enc", k) for k in range(1, groups)]

    factor = 1.0 / math.sqrt(merged_count * groups)
    turned = shape((in_cols, groups * merged_count), kind)
    grad_second, turned = products(
        second_products, factor, features, merged_all, order, in_cols, merged_count, [turned]
    )
    (grad_first,) = products(
        first_products, factor, [turned], grads_all, list(range(groups)), in_cols, merged_count, []
    )
    return (grads[None], grad_first, grad_second)


def solution(mesh):
    return jax.shard_map(
        body,
        mesh=mesh,
        in_specs=(
            P("enc", "roll", None),
            P("enc", "roll"),
            P("enc", None, None),
            P("enc", None, None),
            P(None, "roll"),
        ),
        out_specs=(P("enc", None, "roll"), P("enc", "roll"), P("enc", "roll")),
        check_vma=False,
    )
```
